32 devices in a mesh: groups: 2 (over y), coord: 8 (over z, x), ckpt: 2 (over core).
Axes of the slice: x: 2, y: 2, z: 4, core: 2. Of those that a mesh axis runs over, the one named last changes fastest.
Arguments:
- projection_input: bfloat16 [2, 2, 384, 4096], P('ckpt', 'groups', None, 'coord'), parts along dimension 1, may hold values from -6 to 6
- gate_output_gradient: bfloat16 [2, 2, 14336, 384], P('ckpt', 'groups', 'coord'), parts along dimension 1, may hold values from -0.59765625 to 0.59765625
- up_output_gradient: bfloat16 [2, 2, 14336, 384], P('ckpt', 'groups', 'coord'), parts along dimension 1, may hold values from -0.59765625 to 0.59765625
- hidden: bfloat16 [2, 2, 14336, 384], P('ckpt', 'groups', 'coord'), parts along dimension 1, may hold values from -6 to 6
- down_output_gradient: bfloat16 [2, 2, 384, 4096], P('ckpt', 'groups', None, 'coord'), parts along dimension 1, may hold values from -0.59765625 to 0.59765625
- gate_adapter_first: bfloat16 [2, 4096, 128], P('ckpt', 'coord'), may hold values from -0.09375 to 0.09375
- gate_adapter_second: bfloat16 [2, 14336, 128], P('ckpt', 'coord'), may hold values from -0.5 to 0.5
- up_adapter_first: bfloat16 [2, 4096, 128], P('ckpt', 'coord'), may hold values from -0.09375 to 0.09375
- up_adapter_second: bfloat16 [2, 14336, 128], P('ckpt', 'coord'), may hold values from -0.5 to 0.5
- down_adapter_first: bfloat16 [2, 14336, 128], P('ckpt', 'coord'), may hold values from -0.046875 to 0.046875
- down_adapter_second: bfloat16 [2, 4096, 128], P('ckpt', 'coord'), may hold values from -0.5 to 0.5
- random_sign_flags: int32 [16777216], P(('coord', 'ckpt')), may hold values 0 or 1
- sampled_coordinate_index: int32 [8192], replicated, may hold values from 0 to 16777215
Outputs:
- features: float32 [2, 8192], P('groups'), parts along dimension 0
The draws below stay inside these ranges and needn't reach their ends.
There are 2 independent parts, one for each index of `groups`. The reference program is written for one: setup_inputs(seed, part) draws one part's arguments, and reference() takes and returns one part's arrays. A program takes and returns all parts, laid end to end along the dimension named above; an argument that names none is the same for every part. Nothing has to cross between parts.
All inputs are finite; a program needn't handle non-finite values. No bound on the sum of `random_sign_flags` on one device may be relied on, other than what follows from the above.
Results may differ from the reference program's by a relative error of at most 0.0031.
Values may be sent and summed in bfloat16 or wider, within the bound.
A program may use at most 64 MiB of HBM per device.

```python
import jax
import jax.numpy as jnp

MODEL_WIDTH = 4096
HIDDEN_UNITS = 14336
ADAPTER_RANK = 128
HAD = 16777216
K = 8192
SEQ = 384
EX = 1
LOC = 1048576
N_COORD = 8


def place_ends(entries, rng, least, largest):
    place = [jax.random.randint(jax.random.fold_in(rng, axis), (), 0, length) for axis, length in enumerate(entries.shape)]
    widest = entries.shape.index(max(entries.shape))
    next_to = place[:widest] + [(place[widest] + 1) % entries.shape[widest]] + place[widest + 1:]
    return entries.at[tuple(place)].set(least).at[tuple(next_to)].set(largest)


def levels(key, shape, cuts, smallest, top_value):
    level, own = 1.0, jax.random.fold_in(key, 6)
    for position, shards_of in cuts:
        heights = jnp.exp(jax.random.uniform(jax.random.fold_in(own, position), (shards_of,), jnp.float32, smallest / len(cuts), top_value / len(cuts)))
        level = level * jnp.repeat(heights, shape[position] // shards_of).reshape([-1 if axis == position else 1 for axis in range(len(shape))])
    return level


def scatter_about(own_key, shape, spread, reach, cuts=(), dtype=jnp.bfloat16):
    gain = levels(own_key, shape, cuts, -0.22, 0.18) if cuts else 1.0
    entries = jax.random.normal(own_key, shape, jnp.float32) * spread * gain
    return jnp.minimum(jnp.maximum(entries, -reach), reach).astype(dtype)


def setup_inputs(seed: int = 0, part: int = 0) -> dict:
    splits = jax.random.split(jax.random.key(seed), 14)
    own_keys = jax.random.split(jax.random.fold_in(splits[13], part), 14)
    projection_input = scatter_about(own_keys[0], (2, EX, SEQ, MODEL_WIDTH), 1.0, 6.0, ((0, 2), (3, 8)))
    gate_output_gradient = scatter_about(own_keys[1], (2, EX, HIDDEN_UNITS, SEQ), 0.1, 0.59765625, ((0, 2), (2, 8)))
    up_output_gradient = scatter_about(own_keys[2], (2, EX, HIDDEN_UNITS, SEQ), 0.1, 0.59765625, ((0, 2), (2, 8)))
    hidden = scatter_about(own_keys[3], (2, EX, HIDDEN_UNITS, SEQ), 1.0, 6.0, ((0, 2), (2, 8)))
    down_output_gradient = scatter_about(own_keys[4], (2, EX, SEQ, MODEL_WIDTH), 0.1, 0.59765625, ((0, 2), (3, 8)))
    gate_adapter_first = scatter_about(splits[5], (2, MODEL_WIDTH, ADAPTER_RANK), MODEL_WIDTH ** -0.5, 0.09375, ((0, 2), (1, 8)))
    gate_adapter_second = scatter_about(splits[6], (2, HIDDEN_UNITS, ADAPTER_RANK), ADAPTER_RANK ** -0.5, 0.5, ((0, 2), (1, 8)))
    up_adapter_first = scatter_about(splits[7], (2, MODEL_WIDTH, ADAPTER_RANK), MODEL_WIDTH ** -0.5, 0.09375, ((0, 2), (1, 8)))
    up_adapter_second = scatter_about(splits[8], (2, HIDDEN_UNITS, ADAPTER_RANK), ADAPTER_RANK ** -0.5, 0.5, ((0, 2), (1, 8)))
    down_adapter_first = scatter_about(splits[9], (2, HIDDEN_UNITS, ADAPTER_RANK), HIDDEN_UNITS ** -0.5, 0.046875, ((0, 2), (1, 8)))
    down_adapter_second = scatter_about(splits[10], (2, MODEL_WIDTH, ADAPTER_RANK), ADAPTER_RANK ** -0.5, 0.5, ((0, 2), (1, 8)))
    random_sign_flags = place_ends((jax.random.randint(splits[11], (HAD,), 0, 2) < 1).astype(jnp.int32), jax.random.fold_in(splits[11], 1), 0, 1)
    sampled_coordinate_index = place_ends(jax.random.randint(splits[12], (K,), 0, HAD), jax.random.fold_in(splits[12], 1), 0, HAD - 1).astype(jnp.int32)
    return dict(projection_input=projection_input, gate_output_gradient=gate_output_gradient, up_output_gradient=up_output_gradient, hidden=hidden, down_output_gradient=down_output_gradient, gate_adapter_first=gate_adapter_first, gate_adapter_second=gate_adapter_second, up_adapter_first=up_adapter_first, up_adapter_second=up_adapter_second, down_adapter_first=down_adapter_first, down_adapter_second=down_adapter_second, random_sign_flags=random_sign_flags, sampled_coordinate_index=sampled_coordinate_index)


adapter_scale = 2.0


def cast_to_single_float(array):
    return array.astype(jnp.float32)


def cast_to_brain_float(array):
    return array.astype(jnp.bfloat16)


def walsh_full(vector):
    length = vector.shape[0]
    stride = 1
    while stride < length:
        pieces = vector.reshape(length // (2 * stride), 2, stride)
        vector = jnp.stack([pieces[:, 0] + pieces[:, 1], pieces[:, 0] - pieces[:, 1]], axis=1).reshape(length)
        stride = stride * 2
    return vector


def blocks(matrix):
    return matrix.reshape(matrix.shape[0], N_COORD, matrix.shape[1] // N_COORD, matrix.shape[2])


def reference(projection_input, gate_output_gradient, up_output_gradient, hidden, down_output_gradient, gate_adapter_first, gate_adapter_second, up_adapter_first, up_adapter_second, down_adapter_first, down_adapter_second, random_sign_flags, sampled_coordinate_index):
    columns = []
    for ensemble_member in range(2):
        input_tensors = cast_to_single_float(projection_input[ensemble_member])
        gate_cotangent_value = cast_to_single_float(gate_output_gradient[ensemble_member])
        up_cotangent_value = cast_to_single_float(up_output_gradient[ensemble_member])
        hidden_input_rows = cast_to_single_float(hidden[ensemble_member])
        output_cotangent_value = cast_to_single_float(down_output_gradient[ensemble_member])
        gate_forward_pass = cast_to_brain_float(jnp.einsum('nuj,jx->nux', input_tensors, cast_to_single_float(gate_adapter_first[ensemble_member])))
        up_forward_pass = cast_to_brain_float(jnp.einsum('nuj,jx->nux', input_tensors, cast_to_single_float(up_adapter_first[ensemble_member])))
        down_forward_pass = cast_to_brain_float(jnp.einsum('udo,da->uoa', hidden_input_rows, cast_to_single_float(down_adapter_first[ensemble_member])))
        gate_backward_pass = cast_to_brain_float(jnp.einsum('udo,da->uoa', gate_cotangent_value, cast_to_single_float(gate_adapter_second[ensemble_member])))
        up_backward_pass = cast_to_brain_float(jnp.einsum('udo,da->uoa', up_cotangent_value, cast_to_single_float(up_adapter_second[ensemble_member])))
        down_backward_pass = cast_to_brain_float(jnp.einsum('nuj,jx->nux', output_cotangent_value, cast_to_single_float(down_adapter_second[ensemble_member])))
        gate_adapter_a_gradient = adapter_scale * jnp.einsum('ktv,ktj->kvj', input_tensors, cast_to_single_float(gate_backward_pass))
        up_adapter_a_gradient = adapter_scale * jnp.einsum('ktv,ktj->kvj', input_tensors, cast_to_single_float(up_backward_pass))
        down_adapter_b_gradient = adapter_scale * jnp.einsum('ktv,ktj->kvj', output_cotangent_value, cast_to_single_float(down_forward_pass))
        gate_adapter_b_gradient = adapter_scale * jnp.einsum('jpx,jxg->jpg', gate_cotangent_value, cast_to_single_float(gate_forward_pass))
        up_adapter_b_gradient = adapter_scale * jnp.einsum('jpx,jxg->jpg', up_cotangent_value, cast_to_single_float(up_forward_pass))
        down_adapter_a_gradient = adapter_scale * jnp.einsum('jpx,jxg->jpg', hidden_input_rows, cast_to_single_float(down_backward_pass))
        padding = jnp.zeros((EX, N_COORD, LOC // ADAPTER_RANK - 3 * (MODEL_WIDTH + HIDDEN_UNITS) // N_COORD, ADAPTER_RANK), jnp.float32)
        columns.append(jnp.concatenate([blocks(gate_adapter_a_gradient), blocks(up_adapter_a_gradient), blocks(down_adapter_b_gradient), blocks(gate_adapter_b_gradient), blocks(up_adapter_b_gradient), blocks(down_adapter_a_gradient), padding], axis=2))
    joined = jnp.stack(columns, axis=2).reshape(EX, HAD)
    signed = joined * (1.0 - 2.0 * cast_to_single_float(random_sign_flags))[None, :]
    row_list = []
    for prompt in range(EX):
        row_list.append(walsh_full(signed[prompt])[sampled_coordinate_index])
    return jnp.stack(row_list) * (float(HAD) ** -0.5)
```

```python
import functools

import jax
import jax.numpy as jnp
from jax import lax
from jax.experimental import pallas as pl
from jax.experimental.pallas import tpu as pltpu
from jax.sharding import PartitionSpec as P

ADAPTER_SCALE = 2.0


def matrix_product(form, left, right):
    return jnp.einsum(form, left, right, preferred_element_type=jnp.float32)


def walsh_signs(rows, columns):
    shape = (rows, columns)
    i = lax.broadcasted_iota(jnp.int32, shape, 0)
    j = lax.broadcasted_iota(jnp.int32, shape, 1)
    return 1 - 2 * (lax.population_count(i & j) & 1)


def halves(value):
    high = value.astype(jnp.bfloat16)
    return high, (value - high.astype(jnp.float32)).astype(jnp.bfloat16)


def dot(left, right, dims=((1,), (0,))):
    return lax.dot_general(left, right, (dims, ((), ())), preferred_element_type=jnp.float32)


def butterflies(values):
    stride = 1
    while stride < len(values):
        result = list(values)
        for p in range(len(values)):
            if p & stride:
                continue
            a, b = values[p], values[p + stride]
            if b is None:
                result[p], result[p + stride] = a, a
            elif a is None:
                result[p], result[p + stride] = b, -b
            else:
                result[p], result[p + stride] = a + b, a - b
        values, stride = result, 2 * stride
    return values


def project_kernel(
    block_rows,
    chunk,
    row_ref,
    x_ref,
    gg_ref,
    gu_ref,
    h_ref,
    go_ref,
    products_ref,
    flags_ref,
    index_ref,
    out_ref,
    z_ref,
    picked_ref,
):
    total_rows, lanes = z_ref.shape
    width, deep = x_ref.shape[1], gg_ref.shape[0]
    gate_fwd, up_fwd, down_fwd, gate_back, up_back, down_back = range(6)

    row = 0
    for ref, which in ((x_ref, gate_back), (x_ref, up_back), (go_ref, down_fwd)):
        z_ref[pl.ds(row, width), :] = dot(ref[...], products_ref[which], ((0,), (0,)))
        row += width
    for ref, which in ((gg_ref, gate_fwd), (gu_ref, up_fwd), (h_ref, down_back)):
        z_ref[pl.ds(row, deep), :] = dot(ref[...], products_ref[which])
        row += deep
    filled = row
    count = total_rows // block_rows
    used = -(-filled // block_rows)
    if used * block_rows > filled:
        z_ref[pl.ds(filled, used * block_rows - filled), :] = jnp.zeros(
            (used * block_rows - filled, lanes), jnp.float32
        )

    lane_table = walsh_signs(lanes, lanes).astype(jnp.float32).astype(jnp.bfloat16)
    lane_table = jnp.concatenate([lane_table, lane_table], axis=0)
    row_table = walsh_signs(block_rows, block_rows).astype(jnp.float32).astype(jnp.bfloat16)
    row_table = jnp.concatenate([row_table, row_table], axis=1)

    def one_block(b, carry):
        rows = pl.ds(pl.multiple_of(b * block_rows, block_rows), block_rows)
        value = z_ref[rows, :]
        value = jnp.where(flags_ref[rows, :] != 0, -value, value)
        value = dot(jnp.concatenate(halves(value), axis=1), lane_table)
        value = dot(row_table, jnp.concatenate(halves(value), axis=0))
        z_ref[rows, :] = value
        return carry

    lax.fori_loop(0, used, one_block, 0, unroll=3 if used % 3 == 0 else 1)

    def across(r, carry):
        rows = [
            pl.ds(pl.multiple_of(b * block_rows + r * 8, 8), 8) for b in range(count)
        ]
        values = butterflies(
            [z_ref[rows[b], :] if b < used else None for b in range(count)]
        )
        for b in range(count):
            z_ref[rows[b], :] = values[b]
        return carry

    lax.fori_loop(0, block_rows // 8, across, 0)

    def pick(t, carry):
        for k in range(chunk):
            picked_ref[pl.ds(k, 1), :] = z_ref[pl.ds(row_ref[t * chunk + k], 1), :]
        columns = index_ref[pl.ds(t, 1), :] & (lanes - 1)
        turned = picked_ref[...].T
        here = lax.broadcasted_iota(jnp.int32, (lanes, chunk), 0) == columns
        out_ref[pl.ds(t, 1), :] = jnp.sum(jnp.where(here, turned, 0.0), axis=0, keepdims=True)
        return carry

    lax.fori_loop(0, index_ref.shape[0], pick, 0)


def project(x, gg, gu, h, go, products, flags, index):
    lanes = products.shape[2]
    chunk = 128
    total_rows = flags.shape[0] // lanes
    block_rows = min(256, total_rows)
    tiles = index.shape[0] // chunk
    row_of = (index // lanes) % total_rows
    vmem = pl.BlockSpec(memory_space=pltpu.VMEM)
    return pl.pallas_call(
        functools.partial(project_kernel, block_rows, chunk),
        out_shape=jax.ShapeDtypeStruct((tiles, chunk), jnp.float32),
        in_specs=[pl.BlockSpec(memory_space=pltpu.SMEM)] + [vmem] * 8,
        out_specs=vmem,
        scratch_shapes=[
            pltpu.VMEM((total_rows, lanes), jnp.float32),
            pltpu.VMEM((chunk, lanes), jnp.float32),
        ],
        compiler_params=pltpu.CompilerParams(vmem_limit_bytes=48 * 1024 * 1024),
    )(row_of, x, gg, gu, h, go, products, flags.reshape(total_rows, lanes), index.reshape(tiles, chunk))


def shards(
    projection_input,
    gate_output_gradient,
    up_output_gradient,
    hidden,
    down_output_gradient,
    gate_adapter_first,
    gate_adapter_second,
    up_adapter_first,
    up_adapter_second,
    down_adapter_first,
    down_adapter_second,
    random_sign_flags,
    sampled_coordinate_index,
):
    x, go = projection_input[0, 0], down_output_gradient[0, 0]
    gg, gu, h = gate_output_gradient[0, 0], up_output_gradient[0, 0], hidden[0, 0]
    partials = jnp.stack(
        [
            matrix_product("uj,jx->ux", x, gate_adapter_first[0]),
            matrix_product("uj,jx->ux", x, up_adapter_first[0]),
            matrix_product("do,da->oa", h, down_adapter_first[0]),
            matrix_product("do,da->oa", gg, gate_adapter_second[0]),
            matrix_product("do,da->oa", gu, up_adapter_second[0]),
            matrix_product("uj,jx->ux", go, down_adapter_second[0]),
        ]
    )
    products = lax.psum(partials, "coord").astype(jnp.bfloat16)
    kept = project(x, gg, gu, h, go, products, random_sign_flags, sampled_coordinate_index)
    local_len = random_sign_flags.shape[0]
    block_count = lax.axis_size("coord") * lax.axis_size("ckpt")
    me = lax.axis_index("coord") * lax.axis_size("ckpt") + lax.axis_index("ckpt")
    parity = lax.population_count((sampled_coordinate_index // local_len) & me) & 1
    scale = ADAPTER_SCALE * float(local_len * block_count) ** (-0.5)
    kept = jnp.where(parity.reshape(kept.shape) != 0, -scale, scale) * kept
    return lax.psum(kept, ("coord", "ckpt")).reshape(1, -1)


def solution(mesh):
    in_specs = (
        P("ckpt", "groups", None, "coord"),
        P("ckpt", "groups", "coord", None),
        P("ckpt", "groups", "coord", None),
        P("ckpt", "groups", "coord", None),
        P("ckpt", "groups", None, "coord"),
        P("ckpt", "coord", None),
        P("ckpt", "coord", None),
        P("ckpt", "coord", None),
        P("ckpt", "coord", None),
        P("ckpt", "coord", None),
        P("ckpt", "coord", None),
        P(("coord", "ckpt")),
        P(),
    )
    out_specs = P("groups", None)
    return jax.shard_map(shards, mesh=mesh, in_specs=in_specs, out_specs=out_specs, check_vma=False)
```

```python
import functools

import jax
import jax.numpy as jnp
from jax import lax
from jax.experimental import pallas as pl
from jax.experimental.pallas import tpu as pltpu
from jax.sharding import PartitionSpec as P

ADAPTER_SCALE = 2.0


def matrix_product(form, left, right):
    return jnp.einsum(form, left, right, preferred_element_type=jnp.float32)


def walsh_signs(rows, columns):
    shape = (rows, columns)
    i = lax.broadcasted_iota(jnp.int32, shape, 0)
    j = lax.broadcasted_iota(jnp.int32, shape, 1)
    return 1 - 2 * (lax.population_count(i & j) & 1)


def halves(value):
    high = value.astype(jnp.bfloat16)
    return high, (value - high.astype(jnp.float32)).astype(jnp.bfloat16)


def dot(left, right, dims=((1,), (0,))):
    return lax.dot_general(left, right, (dims, ((), ())), preferred_element_type=jnp.float32)


def butterflies(values):
    stride = 1
    while stride < len(values):
        result = list(values)
        for p in range(len(values)):
            if p & stride:
                continue
            a, b = values[p], values[p + stride]
            if b is None:
                result[p], result[p + stride] = a, a
            elif a is None:
                result[p], result[p + stride] = b, -b
            else:
                result[p], result[p + stride] = a + b, a - b
        values, stride = result, 2 * stride
    return values


def project_kernel(
    block_rows,
    chunk,
    row_ref,
    x_ref,
    gg_ref,
    gu_ref,
    h_ref,
    go_ref,
    products_ref,
    flags_ref,
    index_ref,
    out_ref,
    z_ref,
    picked_ref,
):
    total_rows, lanes = z_ref.shape
    width, deep = x_ref.shape[1], gg_ref.shape[0]
    gate_fwd, up_fwd, down_fwd, gate_back, up_back, down_back = range(6)

    row = 0
    for ref, which in ((x_ref, gate_back), (x_ref, up_back), (go_ref, down_fwd)):
        z_ref[pl.ds(row, width), :] = dot(ref[...], products_ref[which], ((0,), (0,)))
        row += width
    for ref, which in ((gg_ref, gate_fwd), (gu_ref, up_fwd), (h_ref, down_back)):
        z_ref[pl.ds(row, deep), :] = dot(ref[...], products_ref[which])
        row += deep
    filled = row
    count = total_rows // block_rows
    used = -(-filled // block_rows)
    if used * block_rows > filled:
        z_ref[pl.ds(filled, used * block_rows - filled), :] = jnp.zeros(
            (used * block_rows - filled, lanes), jnp.float32
        )

    lane_table = walsh_signs(lanes, lanes).astype(jnp.float32).astype(jnp.bfloat16)
    lane_table = jnp.concatenate([lane_table, lane_table], axis=0)
    row_table = walsh_signs(block_rows, block_rows).astype(jnp.float32).astype(jnp.bfloat16)
    row_table = jnp.concatenate([row_table, row_table], axis=1)

    def one_block(b, carry):
        rows = pl.ds(pl.multiple_of(b * block_rows, block_rows), block_rows)
        value = z_ref[rows, :]
        value = jnp.where(flags_ref[rows, :] != 0, -value, value)
        value = dot(jnp.concatenate(halves(value), axis=1), lane_table)
        value = dot(row_table, jnp.concatenate(halves(value), axis=0))
        z_ref[rows, :] = value
        return carry

    lax.fori_loop(0, used, one_block, 0, unroll=3 if used % 3 == 0 else 1)

    def across(r, carry):
        rows = [
            pl.ds(pl.multiple_of(b * block_rows + r * 8, 8), 8) for b in range(count)
        ]
        values = butterflies(
            [z_ref[rows[b], :] if b < used else None for b in range(count)]
        )
        for b in range(count):
            z_ref[rows[b], :] = values[b]
        return carry

    lax.fori_loop(0, block_rows // 8, across, 0)

    def pick(t, carry):
        for k in range(chunk):
            picked_ref[pl.ds(k, 1), :] = z_ref[pl.ds(row_ref[t * chunk + k], 1), :]
        columns = index_ref[pl.ds(t, 1), :] & (lanes - 1)
        turned = picked_ref[...].T
        here = lax.broadcasted_iota(jnp.int32, (lanes, chunk), 0) == columns
        out_ref[pl.ds(t, 1), :] = jnp.sum(jnp.where(here, turned, 0.0), axis=0, keepdims=True)
        return carry

    lax.fori_loop(0, index_ref.shape[0], pick, 0)


def project(x, gg, gu, h, go, products, flags, index):
    lanes = products.shape[2]
    chunk = 128
    total_rows = flags.shape[0] // lanes
    block_rows = min(256, total_rows)
    tiles = index.shape[0] // chunk
    row_of = (index // lanes) % total_rows
    vmem = pl.BlockSpec(memory_space=pltpu.VMEM)
    return pl.pallas_call(
        functools.partial(project_kernel, block_rows, chunk),
        out_shape=jax.ShapeDtypeStruct((tiles, chunk), jnp.float32),
        in_specs=[pl.BlockSpec(memory_space=pltpu.SMEM)] + [vmem] * 8,
        out_specs=vmem,
        scratch_shapes=[
            pltpu.VMEM((total_rows, lanes), jnp.float32),
            pltpu.VMEM((chunk, lanes), jnp.float32),
        ],
        compiler_params=pltpu.CompilerParams(vmem_limit_bytes=48 * 1024 * 1024),
    )(row_of, x, gg, gu, h, go, products, flags.reshape(total_rows, lanes), index.reshape(tiles, chunk))


MESH = pl.DeviceIdType.MESH


def greet(peers):
    barrier = pltpu.get_barrier_semaphore()
    for peer in peers:
        pl.semaphore_signal(barrier, inc=1, device_id=peer, device_id_type=MESH)
    return lambda: pl.semaphore_wait(barrier, len(peers))


def remote(source, target, send, receive, peer):
    return pltpu.make_async_remote_copy(
        src_ref=source,
        dst_ref=target,
        send_sem=send,
        recv_sem=receive,
        device_id=peer,
        device_id_type=MESH,
    )


def products_kernel(
    x_ref, gg_ref, gu_ref, h_ref, go_ref, a1, a2, a3, a4, a5, a6,
    out_ref, part_ref, pair_ref, rest_ref,
    send1, recv1, send2, recv2, send3, recv3, send4, recv4,
):
    count, two, outer, rows, lanes = part_ref.shape
    me = lax.axis_index("coord")
    mine, place = me % two, me // two
    partner = {"coord": place * two + (1 - mine)}
    others = [{"coord": (place + d) % outer * two + mine} for d in range(1, outer)]
    wait_for_all = greet([partner] + others)

    def first(i):
        ref, weights, turned = (
            (x_ref, a1, False),
            (x_ref, a3, False),
            (h_ref, a5, True),
            (gg_ref, a2, True),
            (gu_ref, a4, True),
            (go_ref, a6, False),
        )[i]
        value = dot(ref[...], weights[...], ((0,), (0,)) if turned else ((1,), (0,)))
        part_ref[i] = value.reshape(two, outer, rows, lanes)

    def pair(i):
        return remote(
            part_ref.at[i, 1 - mine], pair_ref.at[i], send1.at[i], recv1.at[i], partner
        )

    def rest(i, d):
        return remote(
            part_ref.at[i, mine, (place + d) % outer],
            rest_ref.at[i, d - 1],
            send2.at[i, d - 1],
            recv2.at[i, d - 1],
            others[d - 1],
        )

    def spread(i, d):
        block = out_ref.at[i, mine, place]
        return remote(block, block, send3.at[i, d - 1], recv3.at[i, d - 1], others[d - 1])

    def finish(i):
        block = out_ref.at[i, mine]
        return remote(block, block, send4.at[i], recv4.at[i], partner)

    order = (0, 1, 5, 3, 4, 2)
    lags = (0, 1, 2, 3)
    for step in range(count + lags[3] + 1):
        if step < count:
            first(order[step])
            if step == 0:
                wait_for_all()
            pair(order[step]).start()
        if 0 <= step - lags[1] < count:
            i = order[step - lags[1]]
            pair(i).wait_recv()
            part_ref[i, mine] += pair_ref[i]
            for d in range(1, outer):
                rest(i, d).start()
        if 0 <= step - lags[2] < count:
            i = order[step - lags[2]]
            total = part_ref[i, mine, place]
            for d in range(1, outer):
                rest(i, d).wait_recv()
                total = total + rest_ref[i, d - 1]
            out_ref[i, mine, place] = total.astype(jnp.bfloat16)
            for d in range(1, outer):
                spread(i, d).start()
        if 0 <= step - lags[3] < count:
            i = order[step - lags[3]]
            for d in range(1, outer):
                spread(i, d).wait_recv()
            finish(i).start()
    for i in order:
        finish(i).wait_recv()
        pair(i).wait_send()
        for d in range(1, outer):
            rest(i, d).wait_send()
            spread(i, d).wait_send()
        finish(i).wait_send()


def products_of(x, gg, gu, h, go, adapters, coord_count):
    seq, lanes = x.shape[0], adapters[0].shape[1]
    two, rows = 2, seq // coord_count
    outer = coord_count // two
    vmem = pl.BlockSpec(memory_space=pltpu.VMEM)
    dma = pltpu.SemaphoreType.DMA
    out = pl.pallas_call(
        products_kernel,
        out_shape=jax.ShapeDtypeStruct((6, two, outer, rows, lanes), jnp.bfloat16),
        in_specs=[vmem] * 11,
        out_specs=vmem,
        scratch_shapes=[
            pltpu.VMEM((6, two, outer, rows, lanes), jnp.float32),
            pltpu.VMEM((6, outer, rows, lanes), jnp.float32),
            pltpu.VMEM((6, outer - 1, rows, lanes), jnp.float32),
            dma((6,)), dma((6,)),
            dma((6, outer - 1)), dma((6, outer - 1)),
            dma((6, outer - 1)), dma((6, outer - 1)),
            dma((6,)), dma((6,)),
        ],
        compiler_params=pltpu.CompilerParams(
            collective_id=0, has_side_effects=True, vmem_limit_bytes=40 * 1024 * 1024
        ),
    )(x, gg, gu, h, go, *adapters)
    return out.reshape(6, seq, lanes)


def total_kernel(members, kept_ref, out_ref, got_ref, send1, recv1, send2, recv2):
    count = kept_ref.shape[0]
    me = lax.axis_index("coord") * members + lax.axis_index("ckpt")
    places = [(me + d) % count for d in range(1, count)]
    peers = [{"coord": p // members, "ckpt": p % members} for p in places]
    greet(peers)()
    scatter = [
        remote(kept_ref.at[places[d]], got_ref.at[d], send1.at[d], recv1.at[d], peers[d])
        for d in range(count - 1)
    ]
    gather = [
        remote(out_ref.at[me], out_ref.at[me], send2.at[d], recv2.at[d], peers[d])
        for d in range(count - 1)
    ]
    for copy in scatter:
        copy.start()
    total = kept_ref[me]
    for d, copy in enumerate(scatter):
        copy.wait_recv()
        total = total + got_ref[d]
    out_ref[me] = total
    for copy in gather:
        copy.start()
    for copy in gather:
        copy.wait_recv()
    for copy in scatter + gather:
        copy.wait_send()


def total_of(kept, count, members):
    shape = (count, kept.size // count // 128, 128)
    vmem = pl.BlockSpec(memory_space=pltpu.VMEM)
    dma = pltpu.SemaphoreType.DMA
    return pl.pallas_call(
        functools.partial(total_kernel, members),
        out_shape=jax.ShapeDtypeStruct(shape, jnp.float32),
        in_specs=[vmem],
        out_specs=vmem,
        scratch_shapes=[pltpu.VMEM((count - 1,) + shape[1:], jnp.float32)]
        + [dma((count - 1,))] * 4,
        compiler_params=pltpu.CompilerParams(collective_id=1, has_side_effects=True),
    )(kept.reshape(shape))


def shards(
    projection_input,
    gate_output_gradient,
    up_output_gradient,
    hidden,
    down_output_gradient,
    gate_adapter_first,
    gate_adapter_second,
    up_adapter_first,
    up_adapter_second,
    down_adapter_first,
    down_adapter_second,
    random_sign_flags,
    sampled_coordinate_index,
):
    x, go = projection_input[0, 0], down_output_gradient[0, 0]
    gg, gu, h = gate_output_gradient[0, 0], up_output_gradient[0, 0], hidden[0, 0]
    coord_count, members = lax.axis_size("coord"), lax.axis_size("ckpt")
    adapters = [
        adapter[0]
        for adapter in (
            gate_adapter_first,
            gate_adapter_second,
            up_adapter_first,
            up_adapter_second,
            down_adapter_first,
            down_adapter_second,
        )
    ]
    if coord_count % 2 == 0 and coord_count <= 32 and x.shape[0] % (16 * coord_count) == 0:
        products = products_of(x, gg, gu, h, go, adapters, coord_count)
    else:
        partials = jnp.stack(
            [
                matrix_product("uj,jx->ux", x, adapters[0]),
                matrix_product("uj,jx->ux", x, adapters[2]),
                matrix_product("do,da->oa", h, adapters[4]),
                matrix_product("do,da->oa", gg, adapters[1]),
                matrix_product("do,da->oa", gu, adapters[3]),
                matrix_product("uj,jx->ux", go, adapters[5]),
            ]
        )
        products = lax.psum(partials, "coord").astype(jnp.bfloat16)
    kept = project(x, gg, gu, h, go, products, random_sign_flags, sampled_coordinate_index)
    local_len = random_sign_flags.shape[0]
    block_count = coord_count * members
    me = lax.axis_index("coord") * members + lax.axis_index("ckpt")
    parity = lax.population_count((sampled_coordinate_index // local_len) & me) & 1
    scale = ADAPTER_SCALE * float(local_len * block_count) ** (-0.5)
    kept = jnp.where(parity.reshape(kept.shape) != 0, -scale, scale) * kept
    if block_count <= 32 and kept.size % (128 * block_count) == 0:
        return total_of(kept, block_count, members).reshape(1, -1)
    return lax.psum(kept, ("coord", "ckpt")).reshape(1, -1)


def solution(mesh):
    in_specs = (
        P("ckpt", "groups", None, "coord"),
        P("ckpt", "groups", "coord", None),
        P("ckpt", "groups", "coord", None),
        P("ckpt", "groups", "coord", None),
        P("ckpt", "groups", None, "coord"),
        P("ckpt", "coord", None),
        P("ckpt", "coord", None),
        P("ckpt", "coord", None),
        P("ckpt", "coord", None),
        P("ckpt", "coord", None),
        P("ckpt", "coord", None),
        P(("coord", "ckpt")),
        P(),
    )
    out_specs = P("groups", None)
    return jax.shard_map(shards, mesh=mesh, in_specs=in_specs, out_specs=out_specs, check_vma=False)
```

```python
import functools

import jax
import jax.numpy as jnp
from jax import lax
from jax.experimental import pallas as pl
from jax.experimental.pallas import tpu as pltpu
from jax.sharding import PartitionSpec as P

ADAPTER_SCALE = 2.0


def matrix_product(form, left, right):
    return jnp.einsum(form, left, right, preferred_element_type=jnp.float32)


def walsh_signs(rows, columns):
    shape = (rows, columns)
    i = lax.broadcasted_iota(jnp.int32, shape, 0)
    j = lax.broadcasted_iota(jnp.int32, shape, 1)
    return 1 - 2 * (lax.population_count(i & j) & 1)


def halves(value):
    high = value.astype(jnp.bfloat16)
    return high, (value - high.astype(jnp.float32)).astype(jnp.bfloat16)


def dot(left, right, dims=((1,), (0,))):
    return lax.dot_general(left, right, (dims, ((), ())), preferred_element_type=jnp.float32)


def butterflies(values):
    stride = 1
    while stride < len(values):
        result = list(values)
        for p in range(len(values)):
            if p & stride:
                continue
            a, b = values[p], values[p + stride]
            if b is None:
                result[p], result[p + stride] = a, a
            elif a is None:
                result[p], result[p + stride] = b, -b
            else:
                result[p], result[p + stride] = a + b, a - b
        values, stride = result, 2 * stride
    return values


def project_kernel(
    block_rows,
    chunk,
    row_ref,
    x_ref,
    gg_ref,
    gu_ref,
    h_ref,
    go_ref,
    products_ref,
    flags_ref,
    index_ref,
    out_ref,
    z_ref,
    picked_ref,
):
    total_rows, lanes = z_ref.shape
    width, deep = x_ref.shape[1], gg_ref.shape[0]
    gate_fwd, up_fwd, down_fwd, gate_back, up_back, down_back = range(6)

    row = 0
    for ref, which in ((x_ref, gate_back), (x_ref, up_back), (go_ref, down_fwd)):
        z_ref[pl.ds(row, width), :] = dot(ref[...], products_ref[which], ((0,), (0,)))
        row += width
    for ref, which in ((gg_ref, gate_fwd), (gu_ref, up_fwd), (h_ref, down_back)):
        z_ref[pl.ds(row, deep), :] = dot(ref[...], products_ref[which])
        row += deep
    filled = row
    count = total_rows // block_rows
    used = -(-filled // block_rows)
    if used * block_rows > filled:
        z_ref[pl.ds(filled, used * block_rows - filled), :] = jnp.zeros(
            (used * block_rows - filled, lanes), jnp.float32
        )

    lane_table = walsh_signs(lanes, lanes).astype(jnp.float32).astype(jnp.bfloat16)
    lane_table = jnp.concatenate([lane_table, lane_table], axis=0)
    row_table = walsh_signs(block_rows, block_rows).astype(jnp.float32).astype(jnp.bfloat16)
    row_table = jnp.concatenate([row_table, row_table], axis=1)

    def one_block(b, carry):
        rows = pl.ds(pl.multiple_of(b * block_rows, block_rows), block_rows)
        value = z_ref[rows, :]
        value = jnp.where(flags_ref[rows, :] != 0, -value, value)
        value = dot(jnp.concatenate(halves(value), axis=1), lane_table)
        value = dot(row_table, jnp.concatenate(halves(value), axis=0))
        z_ref[rows, :] = value
        return carry

    lax.fori_loop(0, used, one_block, 0, unroll=3 if used % 3 == 0 else 1)

    def across(r, carry):
        rows = [
            pl.ds(pl.multiple_of(b * block_rows + r * 8, 8), 8) for b in range(count)
        ]
        values = butterflies(
            [z_ref[rows[b], :] if b < used else None for b in range(count)]
        )
        for b in range(count):
            z_ref[rows[b], :] = values[b]
        return carry

    lax.fori_loop(0, block_rows // 8, across, 0)

    def pick(t, carry):
        for k in range(chunk):
            picked_ref[pl.ds(k, 1), :] = z_ref[pl.ds(row_ref[t * chunk + k], 1), :]
        columns = index_ref[pl.ds(t, 1), :] & (lanes - 1)
        turned = picked_ref[...].T
        here = lax.broadcasted_iota(jnp.int32, (lanes, chunk), 0) == columns
        out_ref[pl.ds(t, 1), :] = jnp.sum(jnp.where(here, turned, 0.0), axis=0, keepdims=True)
        return carry

    lax.fori_loop(0, index_ref.shape[0], pick, 0)


def project(x, gg, gu, h, go, products, flags, index):
    lanes = products.shape[2]
    chunk = 128
    total_rows = flags.shape[0] // lanes
    block_rows = min(256, total_rows)
    tiles = index.shape[0] // chunk
    row_of = (index // lanes) % total_rows
    vmem = pl.BlockSpec(memory_space=pltpu.VMEM)
    return pl.pallas_call(
        functools.partial(project_kernel, block_rows, chunk),
        out_shape=jax.ShapeDtypeStruct((tiles, chunk), jnp.float32),
        in_specs=[pl.BlockSpec(memory_space=pltpu.SMEM)] + [vmem] * 8,
        out_specs=vmem,
        scratch_shapes=[
            pltpu.VMEM((total_rows, lanes), jnp.float32),
            pltpu.VMEM((chunk, lanes), jnp.float32),
        ],
        compiler_params=pltpu.CompilerParams(vmem_limit_bytes=48 * 1024 * 1024),
    )(row_of, x, gg, gu, h, go, products, flags.reshape(total_rows, lanes), index.reshape(tiles, chunk))


MESH = pl.DeviceIdType.MESH


def greet(peers):
    barrier = pltpu.get_barrier_semaphore()
    for peer in peers:
        pl.semaphore_signal(barrier, inc=1, device_id=peer, device_id_type=MESH)
    return lambda: pl.semaphore_wait(barrier, len(peers))


def remote(source, target, send, receive, peer):
    return pltpu.make_async_remote_copy(
        src_ref=source,
        dst_ref=target,
        send_sem=send,
        recv_sem=receive,
        device_id=peer,
        device_id_type=MESH,
    )

def fused_kernel(
    members, block_rows, row_ref, *refs
):
    hbm, (sums_ref,), scratch = refs[:13], refs[13:14], refs[14:]
    local, scratch = scratch[:13], scratch[13:]
    (
        part_ref, pair_ref, rest_ref, out_ref, z_ref, picked_ref, kept_ref, got_ref,
        load, send1, recv1, send2, recv2, send3, recv3, send4, recv4, send5, recv5, send6, recv6,
    ) = scratch
    x_ref, gg_ref, gu_ref, h_ref, go_ref, a1, a2, a3, a4, a5, a6, flags_ref, index_ref = local
    count, two, outer, rows, lanes = part_ref.shape
    members_all = kept_ref.shape[0]
    coord = lax.axis_index("coord")
    mine, place = coord % two, coord // two
    flat = coord * members + lax.axis_index("ckpt")

    loads = [pltpu.make_async_copy(hbm[n], local[n], load.at[n]) for n in range(13)]
    for n in (0, 5, 7, 4, 10, 1, 6, 2, 8, 3, 9, 11, 12):
        loads[n].start()

    def member(d):
        p = (flat + d) % members_all
        return {"coord": p // members, "ckpt": p % members}

    wait_for_all = greet([member(d) for d in range(1, members_all)])
    partner = {"coord": place * two + (1 - mine)}
    others = [{"coord": (place + d) % outer * two + mine} for d in range(1, outer)]

    def first(i):
        n, m, turned = (
            (0, 5, False),
            (0, 7, False),
            (3, 9, True),
            (1, 6, True),
            (2, 8, True),
            (4, 10, False),
        )[i]
        if i != 1:
            loads[n].wait()
        loads[m].wait()
        value = dot(local[n][...], local[m][...], ((0,), (0,)) if turned else ((1,), (0,)))
        part_ref[i] = value.reshape(two, outer, rows, lanes)

    def pair(i):
        return remote(
            part_ref.at[i, 1 - mine], pair_ref.at[i], send1.at[i], recv1.at[i], partner
        )

    def rest(i, d):
        return remote(
            part_ref.at[i, mine, (place + d) % outer],
            rest_ref.at[i, d - 1],
            send2.at[i, d - 1],
            recv2.at[i, d - 1],
            others[d - 1],
        )

    def spread(i, d):
        block = out_ref.at[i, mine, place]
        return remote(block, block, send3.at[i, d - 1], recv3.at[i, d - 1], others[d - 1])

    def finish(i):
        block = out_ref.at[i, mine]
        return remote(block, block, send4.at[i], recv4.at[i], partner)

    def scatter_products(i):
        pair(i).wait_recv()
        part_ref[i, mine] += pair_ref[i]
        for d in range(1, outer):
            rest(i, d).start()

    def sum_products(i):
        total = part_ref[i, mine, place]
        for d in range(1, outer):
            rest(i, d).wait_recv()
            total = total + rest_ref[i, d - 1]
        out_ref[i, mine, place] = total.astype(jnp.bfloat16)
        for d in range(1, outer):
            spread(i, d).start()

    def finish_products(i):
        for d in range(1, outer):
            spread(i, d).wait_recv()
        finish(i).start()

    lane_table = walsh_signs(lanes, lanes).astype(jnp.float32).astype(jnp.bfloat16)
    lane_table = jnp.concatenate([lane_table, lane_table], axis=0)
    row_table = walsh_signs(block_rows, block_rows).astype(jnp.float32).astype(jnp.bfloat16)
    row_table = jnp.concatenate([row_table, row_table], axis=1)
    width, deep = x_ref.shape[1], gg_ref.shape[0]

    def transform(b):
        span = pl.ds(pl.multiple_of(b * block_rows, block_rows), block_rows)
        value = z_ref[span, :]
        value = jnp.where(flags_ref[span, :] != 0, -value, value)
        value = dot(jnp.concatenate(halves(value), axis=1), lane_table)
        return span, dot(row_table, jnp.concatenate(halves(value), axis=0))

    def gradient(i):
        finish(i).wait_recv()
        right = out_ref[i].reshape(two * outer * rows, lanes)
        ref, turned, row = (
            (gg_ref, False, 3 * width),
            (gu_ref, False, 3 * width + deep),
            (go_ref, True, 2 * width),
            (x_ref, True, 0),
            (x_ref, True, width),
            (h_ref, False, 3 * width + 2 * deep),
        )[i]
        size = width if turned else deep
        z_ref[pl.ds(row, size), :] = dot(ref[...], right, ((0,), (0,)) if turned else ((1,), (0,)))
        start, blocks = row // block_rows, size // block_rows

        def some(n, at):
            done = [transform(at + k) for k in range(n)]
            for span, value in done:
                z_ref[span, :] = value

        if blocks >= 2:

            def step(g, carry):
                some(2, start + 2 * g)
                return carry

            lax.fori_loop(0, blocks // 2, step, 0)
        if blocks % 2:
            some(1, start + blocks - 1)

    order = (0, 1, 5, 3, 4, 2)
    for n, i in enumerate(order):
        first(i)
        if n == 0:
            wait_for_all()
        pair(i).start()
    for i in order:
        scatter_products(i)
    for n, i in enumerate(order):
        sum_products(i)
        if n >= 2:
            finish_products(order[n - 2])
    loads[11].wait()
    finish_products(order[4])
    gradient(order[0])
    finish_products(order[5])
    for i in order[1:]:
        gradient(i)

    filled = 3 * (width + deep) // block_rows
    total_blocks = z_ref.shape[0] // block_rows

    def across(r, carry):
        spans = [
            pl.ds(pl.multiple_of(b * block_rows + r * 8, 8), 8) for b in range(total_blocks)
        ]
        values = butterflies(
            [z_ref[spans[b], :] if b < filled else None for b in range(total_blocks)]
        )
        for b in range(total_blocks):
            z_ref[spans[b], :] = values[b]
        return carry

    lax.fori_loop(0, block_rows // 8, across, 0)

    loads[12].wait()
    tiles, chunk = kept_ref.shape[1:]
    local_len = z_ref.shape[0] * lanes
    here = lax.broadcasted_iota(jnp.int32, (lanes, chunk), 0)

    def pick(j):
        for q in range(tiles):
            t = j * tiles + q
            for k in range(chunk):
                picked_ref[q, pl.ds(k, 1), :] = z_ref[pl.ds(row_ref[t * chunk + k], 1), :]
            index = index_ref[pl.ds(j, 1), q, :]
            chosen = jnp.where(here == (index & (lanes - 1)), picked_ref[q].T, 0.0)
            chosen = jnp.sum(chosen, axis=0, keepdims=True)
            odd = lax.population_count((index // local_len) & flat) & 1
            kept_ref[pl.ds(j, 1), q, :] = jnp.where(odd != 0, -chosen, chosen)

    def scatter(d):
        return remote(
            kept_ref.at[(flat + d) % members_all],
            got_ref.at[d - 1],
            send5.at[d - 1],
            recv5.at[d - 1],
            member(d),
        )

    def gather(d):
        return remote(
            sums_ref.at[flat], sums_ref.at[flat], send6.at[d - 1], recv6.at[d - 1], member(d)
        )

    def pick_and_send(d, carry):
        pick((flat + d) % members_all)

        @pl.when(d < members_all)
        def _():
            scatter(d).start()

        return carry

    lax.fori_loop(1, members_all + 1, pick_and_send, 0)
    total = kept_ref[flat]
    for d in range(1, members_all):
        scatter(d).wait_recv()
        total = total + got_ref[d - 1]
    sums_ref[flat] = total
    for d in range(1, members_all):
        gather(d).start()
    for i in order:
        pair(i).wait_send()
        for d in range(1, outer):
            rest(i, d).wait_send()
            spread(i, d).wait_send()
        finish(i).wait_send()
    for d in range(1, members_all):
        gather(d).wait_recv()
        scatter(d).wait_send()
        gather(d).wait_send()


def fused(x, gg, gu, h, go, adapters, flags, index, coord_count, members):
    seq, lanes = x.shape[0], adapters[0].shape[1]
    chunk, block_rows = 128, 256
    total_rows = flags.shape[0] // lanes
    two, rows = 2, seq // coord_count
    outer, everyone = coord_count // two, coord_count * members
    shape = (everyone, index.shape[0] // (everyone * chunk), chunk)
    row_of = (index // lanes) % total_rows
    vmem = pl.BlockSpec(memory_space=pltpu.VMEM)
    dma = pltpu.SemaphoreType.DMA
    arrays = (x, gg, gu, h, go, *adapters, flags.reshape(total_rows, lanes), index.reshape(shape))
    f32 = jnp.float32
    return pl.pallas_call(
        functools.partial(fused_kernel, members, block_rows),
        out_shape=jax.ShapeDtypeStruct(shape, f32),
        in_specs=[pl.BlockSpec(memory_space=pltpu.SMEM)]
        + [pl.BlockSpec(memory_space=pltpu.HBM)] * len(arrays),
        out_specs=vmem,
        scratch_shapes=[pltpu.VMEM(array.shape, array.dtype) for array in arrays]
        + [
            pltpu.VMEM((6, two, outer, rows, lanes), f32),
            pltpu.VMEM((6, outer, rows, lanes), f32),
            pltpu.VMEM((6, outer - 1, rows, lanes), f32),
            pltpu.VMEM((6, two, outer, rows, lanes), jnp.bfloat16),
            pltpu.VMEM((total_rows, lanes), f32),
            pltpu.VMEM((shape[1], chunk, lanes), f32),
            pltpu.VMEM(shape, f32),
            pltpu.VMEM((everyone - 1,) + shape[1:], f32),
            dma((len(arrays),)),
            dma((6,)), dma((6,)),
            dma((6, outer - 1)), dma((6, outer - 1)),
            dma((6, outer - 1)), dma((6, outer - 1)),
            dma((6,)), dma((6,)),
        ]
        + [dma((everyone - 1,))] * 4,
        compiler_params=pltpu.CompilerParams(
            collective_id=0, has_side_effects=True, vmem_limit_bytes=56 * 1024 * 1024
        ),
    )(row_of, *arrays)


def shards(
    projection_input,
    gate_output_gradient,
    up_output_gradient,
    hidden,
    down_output_gradient,
    gate_adapter_first,
    gate_adapter_second,
    up_adapter_first,
    up_adapter_second,
    down_adapter_first,
    down_adapter_second,
    random_sign_flags,
    sampled_coordinate_index,
):
    x, go = projection_input[0, 0], down_output_gradient[0, 0]
    gg, gu, h = gate_output_gradient[0, 0], up_output_gradient[0, 0], hidden[0, 0]
    coord_count, members = lax.axis_size("coord"), lax.axis_size("ckpt")
    adapters = [
        adapter[0]
        for adapter in (
            gate_adapter_first,
            gate_adapter_second,
            up_adapter_first,
            up_adapter_second,
            down_adapter_first,
            down_adapter_second,
        )
    ]
    local_len = random_sign_flags.shape[0]
    block_count = coord_count * members
    scale = ADAPTER_SCALE * float(local_len * block_count) ** (-0.5)
    lanes = adapters[0].shape[1]
    if (
        block_count <= 32
        and coord_count % 2 == 0
        and lanes == 128
        and x.shape[0] % (16 * coord_count) == 0
        and x.shape[1] % 256 == 0
        and gg.shape[0] % 256 == 0
        and sampled_coordinate_index.shape[0] % (128 * block_count) == 0
    ):
        sums = fused(
            x, gg, gu, h, go, adapters, random_sign_flags, sampled_coordinate_index, coord_count, members
        )
        return (scale * sums).reshape(1, -1)
    partials = jnp.stack(
        [
            matrix_product("uj,jx->ux", x, adapters[0]),
            matrix_product("uj,jx->ux", x, adapters[2]),
            matrix_product("do,da->oa", h, adapters[4]),
            matrix_product("do,da->oa", gg, adapters[1]),
            matrix_product("do,da->oa", gu, adapters[3]),
            matrix_product("uj,jx->ux", go, adapters[5]),
        ]
    )
    products = lax.psum(partials, "coord").astype(jnp.bfloat16)
    kept = project(x, gg, gu, h, go, products, random_sign_flags, sampled_coordinate_index)
    me = lax.axis_index("coord") * members + lax.axis_index("ckpt")
    parity = lax.population_count((sampled_coordinate_index // local_len) & me) & 1
    kept = jnp.where(parity.reshape(kept.shape) != 0, -scale, scale) * kept
    return lax.psum(kept, ("coord", "ckpt")).reshape(1, -1)


def solution(mesh):
    in_specs = (
        P("ckpt", "groups", None, "coord"),
        P("ckpt", "groups", "coord", None),
        P("ckpt", "groups", "coord", None),
        P("ckpt", "groups", "coord", None),
        P("ckpt", "groups", None, "coord"),
        P("ckpt", "coord", None),
        P("ckpt", "coord", None),
        P("ckpt", "coord", None),
        P("ckpt", "coord", None),
        P("ckpt", "coord", None),
        P("ckpt", "coord", None),
        P(("coord", "ckpt")),
        P(),
    )
    out_specs = P("groups", None)
    return jax.shard_map(shards, mesh=mesh, in_specs=in_specs, out_specs=out_specs, check_vma=False)
```

```python
import functools

import jax
import jax.numpy as jnp
from jax import lax
from jax.experimental import pallas as pl
from jax.experimental.pallas import tpu as pltpu
from jax.sharding import PartitionSpec as P

ADAPTER_SCALE = 2.0


def matrix_product(form, left, right):
    return jnp.einsum(form, left, right, preferred_element_type=jnp.float32)


def walsh_signs(rows, columns):
    shape = (rows, columns)
    i = lax.broadcasted_iota(jnp.int32, shape, 0)
    j = lax.broadcasted_iota(jnp.int32, shape, 1)
    return 1 - 2 * (lax.population_count(i & j) & 1)


def halves(value):
    high = value.astype(jnp.bfloat16)
    return high, (value - high.astype(jnp.float32)).astype(jnp.bfloat16)


def dot(left, right, dims=((1,), (0,))):
    return lax.dot_general(left, right, (dims, ((), ())), preferred_element_type=jnp.float32)


def butterflies(values):
    stride = 1
    while stride < len(values):
        result = list(values)
        for p in range(len(values)):
            if p & stride:
                continue
            a, b = values[p], values[p + stride]
            if b is None:
                result[p], result[p + stride] = a, a
            elif a is None:
                result[p], result[p + stride] = b, -b
            else:
                result[p], result[p + stride] = a + b, a - b
        values, stride = result, 2 * stride
    return values


def project_kernel(
    block_rows,
    chunk,
    row_ref,
    x_ref,
    gg_ref,
    gu_ref,
    h_ref,
    go_ref,
    products_ref,
    flags_ref,
    index_ref,
    out_ref,
    z_ref,
    picked_ref,
):
    total_rows, lanes = z_ref.shape
    width, deep = x_ref.shape[1], gg_ref.shape[0]
    gate_fwd, up_fwd, down_fwd, gate_back, up_back, down_back = range(6)

    row = 0
    for ref, which in ((x_ref, gate_back), (x_ref, up_back), (go_ref, down_fwd)):
        z_ref[pl.ds(row, width), :] = dot(ref[...], products_ref[which], ((0,), (0,)))
        row += width
    for ref, which in ((gg_ref, gate_fwd), (gu_ref, up_fwd), (h_ref, down_back)):
        z_ref[pl.ds(row, deep), :] = dot(ref[...], products_ref[which])
        row += deep
    filled = row
    count = total_rows // block_rows
    used = -(-filled // block_rows)
    if used * block_rows > filled:
        z_ref[pl.ds(filled, used * block_rows - filled), :] = jnp.zeros(
            (used * block_rows - filled, lanes), jnp.float32
        )

    lane_table = walsh_signs(lanes, lanes).astype(jnp.float32).astype(jnp.bfloat16)
    lane_table = jnp.concatenate([lane_table, lane_table], axis=0)
    row_table = walsh_signs(block_rows, block_rows).astype(jnp.float32).astype(jnp.bfloat16)
    row_table = jnp.concatenate([row_table, row_table], axis=1)

    def one_block(b, carry):
        rows = pl.ds(pl.multiple_of(b * block_rows, block_rows), block_rows)
        value = z_ref[rows, :]
        value = jnp.where(flags_ref[rows, :] != 0, -value, value)
        value = dot(jnp.concatenate(halves(value), axis=1), lane_table)
        value = dot(row_table, jnp.concatenate(halves(value), axis=0))
        z_ref[rows, :] = value
        return carry

    lax.fori_loop(0, used, one_block, 0, unroll=3 if used % 3 == 0 else 1)

    def across(r, carry):
        rows = [
            pl.ds(pl.multiple_of(b * block_rows + r * 8, 8), 8) for b in range(count)
        ]
        values = butterflies(
            [z_ref[rows[b], :] if b < used else None for b in range(count)]
        )
        for b in range(count):
            z_ref[rows[b], :] = values[b]
        return carry

    lax.fori_loop(0, block_rows // 8, across, 0)

    def pick(t, carry):
        for k in range(chunk):
            picked_ref[pl.ds(k, 1), :] = z_ref[pl.ds(row_ref[t * chunk + k], 1), :]
        columns = index_ref[pl.ds(t, 1), :] & (lanes - 1)
        turned = picked_ref[...].T
        here = lax.broadcasted_iota(jnp.int32, (lanes, chunk), 0) == columns
        out_ref[pl.ds(t, 1), :] = jnp.sum(jnp.where(here, turned, 0.0), axis=0, keepdims=True)
        return carry

    lax.fori_loop(0, index_ref.shape[0], pick, 0)


def project(x, gg, gu, h, go, products, flags, index):
    lanes = products.shape[2]
    chunk = 128
    total_rows = flags.shape[0] // lanes
    block_rows = min(256, total_rows)
    tiles = index.shape[0] // chunk
    row_of = (index // lanes) % total_rows
    vmem = pl.BlockSpec(memory_space=pltpu.VMEM)
    return pl.pallas_call(
        functools.partial(project_kernel, block_rows, chunk),
        out_shape=jax.ShapeDtypeStruct((tiles, chunk), jnp.float32),
        in_specs=[pl.BlockSpec(memory_space=pltpu.SMEM)] + [vmem] * 8,
        out_specs=vmem,
        scratch_shapes=[
            pltpu.VMEM((total_rows, lanes), jnp.float32),
            pltpu.VMEM((chunk, lanes), jnp.float32),
        ],
        compiler_params=pltpu.CompilerParams(vmem_limit_bytes=48 * 1024 * 1024),
    )(row_of, x, gg, gu, h, go, products, flags.reshape(total_rows, lanes), index.reshape(tiles, chunk))


MESH = pl.DeviceIdType.MESH


def greet(peers):
    barrier = pltpu.get_barrier_semaphore()
    for peer in peers:
        pl.semaphore_signal(barrier, inc=1, device_id=peer, device_id_type=MESH)
    return lambda: pl.semaphore_wait(barrier, len(peers))


def remote(source, target, send, receive, peer):
    return pltpu.make_async_remote_copy(
        src_ref=source,
        dst_ref=target,
        send_sem=send,
        recv_sem=receive,
        device_id=peer,
        device_id_type=MESH,
    )

def fused_kernel(
    members, block_rows, *refs
):
    hbm, (sums_ref,), scratch = refs[:13], refs[13:14], refs[14:]
    local, scratch = scratch[:13], scratch[13:]
    (
        part_ref, pair_ref, rest_ref, out_ref, z_ref, picked_ref, kept_ref, got_ref,
        load, send1, recv1, send2, recv2, send3, recv3, send4, recv4, send5, recv5, send6, recv6,
        row_ref, fetched, *slots,
    ) = scratch
    x_ref, gg_ref, gu_ref, h_ref, go_ref, a1, a2, a3, a4, a5, a6, flags_ref, index_ref = local
    count, two, outer, rows, lanes = part_ref.shape
    members_all = kept_ref.shape[0]
    coord = lax.axis_index("coord")
    mine, place = coord % two, coord // two
    flat = coord * members + lax.axis_index("ckpt")

    loads = [pltpu.make_async_copy(hbm[n], local[n], load.at[n]) for n in range(13)]
    for n in (0, 5, 7, 4, 10, 1, 6, 2, 8, 3, 9, 11, 12):
        loads[n].start()

    def member(d):
        p = (flat + d) % members_all
        return {"coord": p // members, "ckpt": p % members}

    wait_for_all = greet([member(d) for d in range(1, members_all)])
    partner = {"coord": place * two + (1 - mine)}
    others = [{"coord": (place + d) % outer * two + mine} for d in range(1, outer)]

    def first(i):
        n, m, turned = (
            (0, 5, False),
            (0, 7, False),
            (3, 9, True),
            (1, 6, True),
            (2, 8, True),
            (4, 10, False),
        )[i]
        if i != 1:
            loads[n].wait()
        loads[m].wait()
        value = dot(local[n][...], local[m][...], ((0,), (0,)) if turned else ((1,), (0,)))
        part_ref[i] = value.reshape(two, outer, rows, lanes)

    def pair(i):
        return remote(
            part_ref.at[i, 1 - mine], pair_ref.at[i], send1.at[i], recv1.at[i], partner
        )

    def rest(i, d):
        return remote(
            part_ref.at[i, mine, (place + d) % outer],
            rest_ref.at[i, d - 1],
            send2.at[i, d - 1],
            recv2.at[i, d - 1],
            others[d - 1],
        )

    def spread(i, d):
        block = out_ref.at[i, mine, place]
        return remote(block, block, send3.at[i, d - 1], recv3.at[i, d - 1], others[d - 1])

    def finish(i):
        block = out_ref.at[i, mine]
        return remote(block, block, send4.at[i], recv4.at[i], partner)

    def scatter_products(i):
        pair(i).wait_recv()
        part_ref[i, mine] += pair_ref[i]
        for d in range(1, outer):
            rest(i, d).start()

    def sum_products(i):
        total = part_ref[i, mine, place]
        for d in range(1, outer):
            rest(i, d).wait_recv()
            total = total + rest_ref[i, d - 1]
        out_ref[i, mine, place] = total.astype(jnp.bfloat16)
        for d in range(1, outer):
            spread(i, d).start()

    def finish_products(i):
        for d in range(1, outer):
            spread(i, d).wait_recv()
        finish(i).start()

    lane_table = walsh_signs(lanes, lanes).astype(jnp.float32).astype(jnp.bfloat16)
    lane_table = jnp.concatenate([lane_table, lane_table], axis=0)
    row_table = walsh_signs(block_rows, block_rows).astype(jnp.float32).astype(jnp.bfloat16)
    row_table = jnp.concatenate([row_table, row_table], axis=1)
    width, deep = x_ref.shape[1], gg_ref.shape[0]

    def transform(b):
        span = pl.ds(pl.multiple_of(b * block_rows, block_rows), block_rows)
        value = z_ref[span, :]
        value = jnp.where(flags_ref[span, :] != 0, -value, value)
        value = dot(jnp.concatenate(halves(value), axis=1), lane_table)
        return span, dot(row_table, jnp.concatenate(halves(value), axis=0))

    def gradient(i):
        finish(i).wait_recv()
        right = out_ref[i].reshape(two * outer * rows, lanes)
        ref, turned, row = (
            (gg_ref, False, 3 * width),
            (gu_ref, False, 3 * width + deep),
            (go_ref, True, 2 * width),
            (x_ref, True, 0),
            (x_ref, True, width),
            (h_ref, False, 3 * width + 2 * deep),
        )[i]
        size = width if turned else deep
        z_ref[pl.ds(row, size), :] = dot(ref[...], right, ((0,), (0,)) if turned else ((1,), (0,)))
        start, blocks = row // block_rows, size // block_rows

        def some(n, at):
            done = [transform(at + k) for k in range(n)]
            for span, value in done:
                z_ref[span, :] = value

        if blocks >= 2:

            def step(g, carry):
                some(2, start + 2 * g)
                return carry

            lax.fori_loop(0, blocks // 2, step, 0)
        if blocks % 2:
            some(1, start + blocks - 1)

    order = (0, 1, 5, 3, 4, 2)
    for n, i in enumerate(order):
        first(i)
        if n == 0:
            wait_for_all()
        pair(i).start()
    for i in order:
        scatter_products(i)
    for n, i in enumerate(order):
        sum_products(i)
        if n >= 2:
            finish_products(order[n - 2])
    loads[12].wait()
    row_ref[...] = (index_ref[...] // lanes) % z_ref.shape[0]
    loads[11].wait()
    finish_products(order[4])
    gradient(order[0])
    finish_products(order[5])
    for i in order[1:]:
        gradient(i)

    def fetch(n, d):
        return pltpu.make_async_copy(
            row_ref.at[(flat + d) % members_all], slots[n], fetched.at[n]
        )

    for n in range(len(slots)):
        fetch(n, n + 1).start()

    filled = 3 * (width + deep) // block_rows
    total_blocks = z_ref.shape[0] // block_rows

    def across(r, carry):
        spans = [
            pl.ds(pl.multiple_of(b * block_rows + r * 8, 8), 8) for b in range(total_blocks)
        ]
        values = butterflies(
            [z_ref[spans[b], :] if b < filled else None for b in range(total_blocks)]
        )
        for b in range(total_blocks):
            z_ref[spans[b], :] = values[b]
        return carry

    lax.fori_loop(0, block_rows // 8, across, 0)

    tiles, chunk = kept_ref.shape[1:]
    local_len = z_ref.shape[0] * lanes
    here = lax.broadcasted_iota(jnp.int32, (lanes, chunk), 0)

    def pick(j, slot):
        for q in range(tiles):
            for k in range(chunk):
                picked_ref[q, pl.ds(k, 1), :] = z_ref[pl.ds(slot[q, k], 1), :]
            index = index_ref[pl.ds(j, 1), q, :]
            chosen = jnp.where(here == (index & (lanes - 1)), picked_ref[q].T, 0.0)
            chosen = jnp.sum(chosen, axis=0, keepdims=True)
            odd = lax.population_count((index // local_len) & flat) & 1
            kept_ref[pl.ds(j, 1), q, :] = jnp.where(odd != 0, -chosen, chosen)

    def scatter(d):
        return remote(
            kept_ref.at[(flat + d) % members_all],
            got_ref.at[d - 1],
            send5.at[d - 1],
            recv5.at[d - 1],
            member(d),
        )

    def gather(d):
        return remote(
            sums_ref.at[flat], sums_ref.at[flat], send6.at[d - 1], recv6.at[d - 1], member(d)
        )

    def pick_and_send(g, carry):
        for n in range(len(slots)):
            d = g * len(slots) + n + 1
            fetch(n, d).wait()
            pick((flat + d) % members_all, slots[n])

            @pl.when(d + len(slots) <= members_all)
            def _():
                fetch(n, d + len(slots)).start()

            @pl.when(d < members_all)
            def _():
                scatter(d).start()

        return carry

    lax.fori_loop(0, members_all // len(slots), pick_and_send, 0)
    total = kept_ref[flat]
    for d in range(1, members_all):
        scatter(d).wait_recv()
        total = total + got_ref[d - 1]
    sums_ref[flat] = total
    for d in range(1, members_all):
        gather(d).start()
    for i in order:
        pair(i).wait_send()
        for d in range(1, outer):
            rest(i, d).wait_send()
            spread(i, d).wait_send()
        finish(i).wait_send()
    for d in range(1, members_all):
        gather(d).wait_recv()
        scatter(d).wait_send()
        gather(d).wait_send()


def fused(x, gg, gu, h, go, adapters, flags, index, coord_count, members):
    seq, lanes = x.shape[0], adapters[0].shape[1]
    chunk, block_rows = 128, 256
    total_rows = flags.shape[0] // lanes
    two, rows = 2, seq // coord_count
    outer, everyone = coord_count // two, coord_count * members
    shape = (everyone, index.shape[0] // (everyone * chunk), chunk)
    slots = 4
    vmem = pl.BlockSpec(memory_space=pltpu.VMEM)
    dma = pltpu.SemaphoreType.DMA
    arrays = (x, gg, gu, h, go, *adapters, flags.reshape(total_rows, lanes), index.reshape(shape))
    f32 = jnp.float32
    return pl.pallas_call(
        functools.partial(fused_kernel, members, block_rows),
        out_shape=jax.ShapeDtypeStruct(shape, f32),
        in_specs=[pl.BlockSpec(memory_space=pltpu.HBM)] * len(arrays),
        out_specs=vmem,
        scratch_shapes=[pltpu.VMEM(array.shape, array.dtype) for array in arrays]
        + [
            pltpu.VMEM((6, two, outer, rows, lanes), f32),
            pltpu.VMEM((6, outer, rows, lanes), f32),
            pltpu.VMEM((6, outer - 1, rows, lanes), f32),
            pltpu.VMEM((6, two, outer, rows, lanes), jnp.bfloat16),
            pltpu.VMEM((total_rows, lanes), f32),
            pltpu.VMEM((shape[1], chunk, lanes), f32),
            pltpu.VMEM(shape, f32),
            pltpu.VMEM((everyone - 1,) + shape[1:], f32),
            dma((len(arrays),)),
            dma((6,)), dma((6,)),
            dma((6, outer - 1)), dma((6, outer - 1)),
            dma((6, outer - 1)), dma((6, outer - 1)),
            dma((6,)), dma((6,)),
        ]
        + [dma((everyone - 1,))] * 4
        + [pltpu.VMEM(shape, jnp.int32), dma((slots,))]
        + [pltpu.SMEM(shape[1:], jnp.int32)] * slots,
        compiler_params=pltpu.CompilerParams(
            collective_id=0, has_side_effects=True, vmem_limit_bytes=56 * 1024 * 1024
        ),
    )(*arrays)


def shards(
    projection_input,
    gate_output_gradient,
    up_output_gradient,
    hidden,
    down_output_gradient,
    gate_adapter_first,
    gate_adapter_second,
    up_adapter_first,
    up_adapter_second,
    down_adapter_first,
    down_adapter_second,
    random_sign_flags,
    sampled_coordinate_index,
):
    x, go = projection_input[0, 0], down_output_gradient[0, 0]
    gg, gu, h = gate_output_gradient[0, 0], up_output_gradient[0, 0], hidden[0, 0]
    coord_count, members = lax.axis_size("coord"), lax.axis_size("ckpt")
    adapters = [
        adapter[0]
        for adapter in (
            gate_adapter_first,
            gate_adapter_second,
            up_adapter_first,
            up_adapter_second,
            down_adapter_first,
            down_adapter_second,
        )
    ]
    local_len = random_sign_flags.shape[0]
    block_count = coord_count * members
    scale = ADAPTER_SCALE * float(local_len * block_count) ** (-0.5)
    lanes = adapters[0].shape[1]
    if (
        block_count <= 32
        and block_count % 4 == 0
        and coord_count % 2 == 0
        and lanes == 128
        and x.shape[0] % (16 * coord_count) == 0
        and x.shape[1] % 256 == 0
        and gg.shape[0] % 256 == 0
        and sampled_coordinate_index.shape[0] % (128 * block_count) == 0
    ):
        sums = fused(
            x, gg, gu, h, go, adapters, random_sign_flags, sampled_coordinate_index, coord_count, members
        )
        return (scale * sums).reshape(1, -1)
    partials = jnp.stack(
        [
            matrix_product("uj,jx->ux", x, adapters[0]),
            matrix_product("uj,jx->ux", x, adapters[2]),
            matrix_product("do,da->oa", h, adapters[4]),
            matrix_product("do,da->oa", gg, adapters[1]),
            matrix_product("do,da->oa", gu, adapters[3]),
            matrix_product("uj,jx->ux", go, adapters[5]),
        ]
    )
    products = lax.psum(partials, "coord").astype(jnp.bfloat16)
    kept = project(x, gg, gu, h, go, products, random_sign_flags, sampled_coordinate_index)
    me = lax.axis_index("coord") * members + lax.axis_index("ckpt")
    parity = lax.population_count((sampled_coordinate_index // local_len) & me) & 1
    kept = jnp.where(parity.reshape(kept.shape) != 0, -scale, scale) * kept
    return lax.psum(kept, ("coord", "ckpt")).reshape(1, -1)


def solution(mesh):
    in_specs = (
        P("ckpt", "groups", None, "coord"),
        P("ckpt", "groups", "coord", None),
        P("ckpt", "groups", "coord", None),
        P("ckpt", "groups", "coord", None),
        P("ckpt", "groups", None, "coord"),
        P("ckpt", "coord", None),
        P("ckpt", "coord", None),
        P("ckpt", "coord", None),
        P("ckpt", "coord", None),
        P("ckpt", "coord", None),
        P("ckpt", "coord", None),
        P(("coord", "ckpt")),
        P(),
    )
    out_specs = P("groups", None)
    return jax.shard_map(shards, mesh=mesh, in_specs=in_specs, out_specs=out_specs, check_vma=False)
```

```python
import functools

import jax
import jax.numpy as jnp
from jax import lax
from jax.experimental import pallas as pl
from jax.experimental.pallas import tpu as pltpu
from jax.sharding import PartitionSpec as P

ADAPTER_SCALE = 2.0


def matrix_product(form, left, right):
    return jnp.einsum(form, left, right, preferred_element_type=jnp.float32)


def walsh_signs(rows, columns):
    shape = (rows, columns)
    i = lax.broadcasted_iota(jnp.int32, shape, 0)
    j = lax.broadcasted_iota(jnp.int32, shape, 1)
    return 1 - 2 * (lax.population_count(i & j) & 1)


def halves(value):
    high = value.astype(jnp.bfloat16)
    return high, (value - high.astype(jnp.float32)).astype(jnp.bfloat16)


def dot(left, right, dims=((1,), (0,))):
    return lax.dot_general(left, right, (dims, ((), ())), preferred_element_type=jnp.float32)


def butterflies(values):
    stride = 1
    while stride < len(values):
        result = list(values)
        for p in range(len(values)):
            if p & stride:
                continue
            a, b = values[p], values[p + stride]
            if b is None:
                result[p], result[p + stride] = a, a
            elif a is None:
                result[p], result[p + stride] = b, -b
            else:
                result[p], result[p + stride] = a + b, a - b
        values, stride = result, 2 * stride
    return values


def project_kernel(
    block_rows,
    chunk,
    row_ref,
    x_ref,
    gg_ref,
    gu_ref,
    h_ref,
    go_ref,
    products_ref,
    flags_ref,
    index_ref,
    out_ref,
    z_ref,
    picked_ref,
):
    total_rows, lanes = z_ref.shape
    width, deep = x_ref.shape[1], gg_ref.shape[0]
    gate_fwd, up_fwd, down_fwd, gate_back, up_back, down_back = range(6)

    row = 0
    for ref, which in ((x_ref, gate_back), (x_ref, up_back), (go_ref, down_fwd)):
        z_ref[pl.ds(row, width), :] = dot(ref[...], products_ref[which], ((0,), (0,)))
        row += width
    for ref, which in ((gg_ref, gate_fwd), (gu_ref, up_fwd), (h_ref, down_back)):
        z_ref[pl.ds(row, deep), :] = dot(ref[...], products_ref[which])
        row += deep
    filled = row
    count = total_rows // block_rows
    used = -(-filled // block_rows)
    if used * block_rows > filled:
        z_ref[pl.ds(filled, used * block_rows - filled), :] = jnp.zeros(
            (used * block_rows - filled, lanes), jnp.float32
        )

    lane_table = walsh_signs(lanes, lanes).astype(jnp.float32).astype(jnp.bfloat16)
    lane_table = jnp.concatenate([lane_table, lane_table], axis=0)
    row_table = walsh_signs(block_rows, block_rows).astype(jnp.float32).astype(jnp.bfloat16)
    row_table = jnp.concatenate([row_table, row_table], axis=1)

    def one_block(b, carry):
        rows = pl.ds(pl.multiple_of(b * block_rows, block_rows), block_rows)
        value = z_ref[rows, :]
        value = jnp.where(flags_ref[rows, :] != 0, -value, value)
        value = dot(jnp.concatenate(halves(value), axis=1), lane_table)
        value = dot(row_table, jnp.concatenate(halves(value), axis=0))
        z_ref[rows, :] = value
        return carry

    lax.fori_loop(0, used, one_block, 0, unroll=3 if used % 3 == 0 else 1)

    def across(r, carry):
        rows = [
            pl.ds(pl.multiple_of(b * block_rows + r * 8, 8), 8) for b in range(count)
        ]
        values = butterflies(
            [z_ref[rows[b], :] if b < used else None for b in range(count)]
        )
        for b in range(count):
            z_ref[rows[b], :] = values[b]
        return carry

    lax.fori_loop(0, block_rows // 8, across, 0)

    def pick(t, carry):
        for k in range(chunk):
            picked_ref[pl.ds(k, 1), :] = z_ref[pl.ds(row_ref[t * chunk + k], 1), :]
        columns = index_ref[pl.ds(t, 1), :] & (lanes - 1)
        turned = picked_ref[...].T
        here = lax.broadcasted_iota(jnp.int32, (lanes, chunk), 0) == columns
        out_ref[pl.ds(t, 1), :] = jnp.sum(jnp.where(here, turned, 0.0), axis=0, keepdims=True)
        return carry

    lax.fori_loop(0, index_ref.shape[0], pick, 0)


def project(x, gg, gu, h, go, products, flags, index):
    lanes = products.shape[2]
    chunk = 128
    total_rows = flags.shape[0] // lanes
    block_rows = min(256, total_rows)
    tiles = index.shape[0] // chunk
    row_of = (index // lanes) % total_rows
    vmem = pl.BlockSpec(memory_space=pltpu.VMEM)
    return pl.pallas_call(
        functools.partial(project_kernel, block_rows, chunk),
        out_shape=jax.ShapeDtypeStruct((tiles, chunk), jnp.float32),
        in_specs=[pl.BlockSpec(memory_space=pltpu.SMEM)] + [vmem] * 8,
        out_specs=vmem,
        scratch_shapes=[
            pltpu.VMEM((total_rows, lanes), jnp.float32),
            pltpu.VMEM((chunk, lanes), jnp.float32),
        ],
        compiler_params=pltpu.CompilerParams(vmem_limit_bytes=48 * 1024 * 1024),
    )(row_of, x, gg, gu, h, go, products, flags.reshape(total_rows, lanes), index.reshape(tiles, chunk))


MESH = pl.DeviceIdType.MESH


def greet(peers):
    barrier = pltpu.get_barrier_semaphore()
    for peer in peers:
        pl.semaphore_signal(barrier, inc=1, device_id=peer, device_id_type=MESH)
    return lambda: pl.semaphore_wait(barrier, len(peers))


def remote(source, target, send, receive, peer):
    return pltpu.make_async_remote_copy(
        src_ref=source,
        dst_ref=target,
        send_sem=send,
        recv_sem=receive,
        device_id=peer,
        device_id_type=MESH,
    )

def fused_kernel(
    members, block_rows, *refs
):
    hbm, (sums_ref,), scratch = refs[:13], refs[13:14], refs[14:]
    local, scratch = scratch[:13], scratch[13:]
    (
        part_ref, pair_ref, rest_ref, out_ref, z_ref, picked_ref, kept_ref, got_ref,
        load, send1, recv1, send2, recv2, send3, recv3, send4, recv4, send5, recv5, send6, recv6,
        row_ref, fetched, *slots,
    ) = scratch
    x_ref, gg_ref, gu_ref, h_ref, go_ref, a1, a2, a3, a4, a5, a6, flags_ref, index_ref = local
    count, two, outer, rows, lanes = part_ref.shape
    members_all = kept_ref.shape[0]
    coord = lax.axis_index("coord")
    mine, place = coord % two, coord // two
    flat = coord * members + lax.axis_index("ckpt")

    loads = [pltpu.make_async_copy(hbm[n], local[n], load.at[n]) for n in range(13)]
    for n in (0, 5, 7, 4, 10, 1, 6, 2, 8, 3, 9, 11, 12):
        loads[n].start()

    def member(d):
        p = (flat + d) % members_all
        return {"coord": p // members, "ckpt": p % members}

    wait_for_all = greet([member(d) for d in range(1, members_all)])
    partner = {"coord": place * two + (1 - mine)}
    others = [{"coord": (place + d) % outer * two + mine} for d in range(1, outer)]

    def first(i):
        n, m, turned = (
            (0, 5, False),
            (0, 7, False),
            (3, 9, True),
            (1, 6, True),
            (2, 8, True),
            (4, 10, False),
        )[i]
        if i != 1:
            loads[n].wait()
        loads[m].wait()
        value = dot(local[n][...], local[m][...], ((0,), (0,)) if turned else ((1,), (0,)))
        part_ref[i] = value.reshape(two, outer, rows, lanes)

    def pair(i):
        return remote(
            part_ref.at[i, 1 - mine], pair_ref.at[i], send1.at[i], recv1.at[i], partner
        )

    def rest(i, d):
        return remote(
            part_ref.at[i, mine, (place + d) % outer],
            rest_ref.at[i, d - 1],
            send2.at[i, d - 1],
            recv2.at[i, d - 1],
            others[d - 1],
        )

    def spread(i, d):
        block = out_ref.at[i, mine, place]
        return remote(block, block, send3.at[i, d - 1], recv3.at[i, d - 1], others[d - 1])

    def finish(i):
        block = out_ref.at[i, mine]
        return remote(block, block, send4.at[i], recv4.at[i], partner)

    def scatter_products(i):
        pair(i).wait_recv()
        part_ref[i, mine] += pair_ref[i]
        for d in range(1, outer):
            rest(i, d).start()

    def sum_products(i):
        total = part_ref[i, mine, place]
        for d in range(1, outer):
            rest(i, d).wait_recv()
            total = total + rest_ref[i, d - 1]
        out_ref[i, mine, place] = total.astype(jnp.bfloat16)
        for d in range(1, outer):
            spread(i, d).start()

    def finish_products(i):
        for d in range(1, outer):
            spread(i, d).wait_recv()
        finish(i).start()

    lane_table = walsh_signs(lanes, lanes).astype(jnp.float32).astype(jnp.bfloat16)
    lane_table = jnp.concatenate([lane_table, lane_table], axis=0)
    row_table = walsh_signs(block_rows, block_rows).astype(jnp.float32).astype(jnp.bfloat16)
    row_table = jnp.concatenate([row_table, row_table], axis=1)
    width, deep = x_ref.shape[1], gg_ref.shape[0]

    def transform(b):
        span = pl.ds(pl.multiple_of(b * block_rows, block_rows), block_rows)
        value = z_ref[span, :]
        value = jnp.where(flags_ref[span, :] != 0, -value, value)
        return span, dot(jnp.concatenate(halves(value), axis=1), lane_table)

    def gradient(i):
        finish(i).wait_recv()
        right = out_ref[i].reshape(two * outer * rows, lanes)
        ref, turned, row = (
            (gg_ref, False, 3 * width),
            (gu_ref, False, 3 * width + deep),
            (go_ref, True, 2 * width),
            (x_ref, True, 0),
            (x_ref, True, width),
            (h_ref, False, 3 * width + 2 * deep),
        )[i]
        size = width if turned else deep
        z_ref[pl.ds(row, size), :] = dot(ref[...], right, ((0,), (0,)) if turned else ((1,), (0,)))
        start, blocks = row // block_rows, size // block_rows

        def some(n, at):
            done = [transform(at + k) for k in range(n)]
            value = jnp.concatenate([value for _, value in done], axis=1)
            value = dot(row_table, jnp.concatenate(halves(value), axis=0))
            for k, (span, _) in enumerate(done):
                z_ref[span, :] = value[:, k * lanes : (k + 1) * lanes]

        if blocks >= 2:

            def step(g, carry):
                some(2, start + 2 * g)
                return carry

            lax.fori_loop(0, blocks // 2, step, 0)
        if blocks % 2:
            some(1, start + blocks - 1)

    order = (0, 1, 5, 3, 4, 2)
    for n, i in enumerate(order):
        first(i)
        if n == 0:
            wait_for_all()
        pair(i).start()
    for i in order:
        scatter_products(i)
    for n, i in enumerate(order):
        sum_products(i)
        if n >= 2:
            finish_products(order[n - 2])
    loads[12].wait()
    row_ref[...] = (index_ref[...] // lanes) % z_ref.shape[0]
    loads[11].wait()
    finish_products(order[4])
    gradient(order[0])
    finish_products(order[5])
    for i in order[1:]:
        gradient(i)

    def fetch(n, d):
        return pltpu.make_async_copy(
            row_ref.at[(flat + d) % members_all], slots[n], fetched.at[n]
        )

    for n in range(len(slots)):
        fetch(n, n + 1).start()

    filled = 3 * (width + deep) // block_rows
    total_blocks = z_ref.shape[0] // block_rows

    def across(r, carry):
        spans = [
            pl.ds(pl.multiple_of(b * block_rows + r * 8, 8), 8) for b in range(total_blocks)
        ]
        values = butterflies(
            [z_ref[spans[b], :] if b < filled else None for b in range(total_blocks)]
        )
        for b in range(total_blocks):
            z_ref[spans[b], :] = values[b]
        return carry

    lax.fori_loop(0, block_rows // 8, across, 0)

    tiles, chunk = kept_ref.shape[1:]
    local_len = z_ref.shape[0] * lanes
    here = lax.broadcasted_iota(jnp.int32, (lanes, chunk), 0)

    def pick(j, slot):
        for q in range(tiles):
            for k in range(chunk):
                picked_ref[q, pl.ds(k, 1), :] = z_ref[pl.ds(slot[q, k], 1), :]
            index = index_ref[pl.ds(j, 1), q, :]
            chosen = jnp.where(here == (index & (lanes - 1)), picked_ref[q].T, 0.0)
            chosen = jnp.sum(chosen, axis=0, keepdims=True)
            odd = lax.population_count((index // local_len) & flat) & 1
            kept_ref[pl.ds(j, 1), q, :] = jnp.where(odd != 0, -chosen, chosen)

    def scatter(d):
        return remote(
            kept_ref.at[(flat + d) % members_all],
            got_ref.at[d - 1],
            send5.at[d - 1],
            recv5.at[d - 1],
            member(d),
        )

    def gather(d):
        return remote(
            sums_ref.at[flat], sums_ref.at[flat], send6.at[d - 1], recv6.at[d - 1], member(d)
        )

    def pick_and_send(g, carry):
        for n in range(len(slots)):
            d = g * len(slots) + n + 1
            fetch(n, d).wait()
            pick((flat + d) % members_all, slots[n])

            @pl.when(d + len(slots) <= members_all)
            def _():
                fetch(n, d + len(slots)).start()

            @pl.when(d < members_all)
            def _():
                scatter(d).start()

        return carry

    lax.fori_loop(0, members_all // len(slots), pick_and_send, 0)
    total = kept_ref[flat]
    for d in range(1, members_all):
        scatter(d).wait_recv()
        total = total + got_ref[d - 1]
    sums_ref[flat] = total
    for d in range(1, members_all):
        gather(d).start()
    for i in order:
        pair(i).wait_send()
        for d in range(1, outer):
            rest(i, d).wait_send()
            spread(i, d).wait_send()
        finish(i).wait_send()
    for d in range(1, members_all):
        gather(d).wait_recv()
        scatter(d).wait_send()
        gather(d).wait_send()


def fused(x, gg, gu, h, go, adapters, flags, index, coord_count, members):
    seq, lanes = x.shape[0], adapters[0].shape[1]
    chunk, block_rows = 128, 256
    total_rows = flags.shape[0] // lanes
    two, rows = 2, seq // coord_count
    outer, everyone = coord_count // two, coord_count * members
    shape = (everyone, index.shape[0] // (everyone * chunk), chunk)
    slots = 4
    vmem = pl.BlockSpec(memory_space=pltpu.VMEM)
    dma = pltpu.SemaphoreType.DMA
    arrays = (x, gg, gu, h, go, *adapters, flags.reshape(total_rows, lanes), index.reshape(shape))
    f32 = jnp.float32
    return pl.pallas_call(
        functools.partial(fused_kernel, members, block_rows),
        out_shape=jax.ShapeDtypeStruct(shape, f32),
        in_specs=[pl.BlockSpec(memory_space=pltpu.HBM)] * len(arrays),
        out_specs=vmem,
        scratch_shapes=[pltpu.VMEM(array.shape, array.dtype) for array in arrays]
        + [
            pltpu.VMEM((6, two, outer, rows, lanes), f32),
            pltpu.VMEM((6, outer, rows, lanes), f32),
            pltpu.VMEM((6, outer - 1, rows, lanes), f32),
            pltpu.VMEM((6, two, outer, rows, lanes), jnp.bfloat16),
            pltpu.VMEM((total_rows, lanes), f32),
            pltpu.VMEM((shape[1], chunk, lanes), f32),
            pltpu.VMEM(shape, f32),
            pltpu.VMEM((everyone - 1,) + shape[1:], f32),
            dma((len(arrays),)),
            dma((6,)), dma((6,)),
            dma((6, outer - 1)), dma((6, outer - 1)),
            dma((6, outer - 1)), dma((6, outer - 1)),
            dma((6,)), dma((6,)),
        ]
        + [dma((everyone - 1,))] * 4
        + [pltpu.VMEM(shape, jnp.int32), dma((slots,))]
        + [pltpu.SMEM(shape[1:], jnp.int32)] * slots,
        compiler_params=pltpu.CompilerParams(
            collective_id=0, has_side_effects=True, vmem_limit_bytes=56 * 1024 * 1024
        ),
    )(*arrays)


def shards(
    projection_input,
    gate_output_gradient,
    up_output_gradient,
    hidden,
    down_output_gradient,
    gate_adapter_first,
    gate_adapter_second,
    up_adapter_first,
    up_adapter_second,
    down_adapter_first,
    down_adapter_second,
    random_sign_flags,
    sampled_coordinate_index,
):
    x, go = projection_input[0, 0], down_output_gradient[0, 0]
    gg, gu, h = gate_output_gradient[0, 0], up_output_gradient[0, 0], hidden[0, 0]
    coord_count, members = lax.axis_size("coord"), lax.axis_size("ckpt")
    adapters = [
        adapter[0]
        for adapter in (
            gate_adapter_first,
            gate_adapter_second,
            up_adapter_first,
            up_adapter_second,
            down_adapter_first,
            down_adapter_second,
        )
    ]
    local_len = random_sign_flags.shape[0]
    block_count = coord_count * members
    scale = ADAPTER_SCALE * float(local_len * block_count) ** (-0.5)
    lanes = adapters[0].shape[1]
    if (
        block_count <= 32
        and block_count % 4 == 0
        and coord_count % 2 == 0
        and lanes == 128
        and x.shape[0] % (16 * coord_count) == 0
        and x.shape[1] % 256 == 0
        and gg.shape[0] % 256 == 0
        and sampled_coordinate_index.shape[0] % (128 * block_count) == 0
    ):
        sums = fused(
            x, gg, gu, h, go, adapters, random_sign_flags, sampled_coordinate_index, coord_count, members
        )
        return (scale * sums).reshape(1, -1)
    partials = jnp.stack(
        [
            matrix_product("uj,jx->ux", x, adapters[0]),
            matrix_product("uj,jx->ux", x, adapters[2]),
            matrix_product("do,da->oa", h, adapters[4]),
            matrix_product("do,da->oa", gg, adapters[1]),
            matrix_product("do,da->oa", gu, adapters[3]),
            matrix_product("uj,jx->ux", go, adapters[5]),
        ]
    )
    products = lax.psum(partials, "coord").astype(jnp.bfloat16)
    kept = project(x, gg, gu, h, go, products, random_sign_flags, sampled_coordinate_index)
    me = lax.axis_index("coord") * members + lax.axis_index("ckpt")
    parity = lax.population_count((sampled_coordinate_index // local_len) & me) & 1
    kept = jnp.where(parity.reshape(kept.shape) != 0, -scale, scale) * kept
    return lax.psum(kept, ("coord", "ckpt")).reshape(1, -1)


def solution(mesh):
    in_specs = (
        P("ckpt", "groups", None, "coord"),
        P("ckpt", "groups", "coord", None),
        P("ckpt", "groups", "coord", None),
        P("ckpt", "groups", "coord", None),
        P("ckpt", "groups", None, "coord"),
        P("ckpt", "coord", None),
        P("ckpt", "coord", None),
        P("ckpt", "coord", None),
        P("ckpt", "coord", None),
        P("ckpt", "coord", None),
        P("ckpt", "coord", None),
        P(("coord", "ckpt")),
        P(),
    )
    out_specs = P("groups", None)
    return jax.shard_map(shards, mesh=mesh, in_specs=in_specs, out_specs=out_specs, check_vma=False)
```
